256 devices in a mesh: samples: 256 (over y, z, x, core).
Axes of the slice: x: 4, y: 4, z: 8, core: 2. Of those that a mesh axis runs over, the one named last changes fastest.
Arguments:
- spin_configs: int32 [256, 256], P('samples'), may hold values from -1 to 1, as said below
- energy: float32 [256], P('samples'), may hold values from -6 to 6
- embedding: float32 [9, 64], replicated, may hold values from -2 to 2
- kernels: float32 [24, 9, 64, 64], replicated, may hold values from -0.25 to 0.25
- readout: float32 [64], replicated, may hold values from -0.75 to 0.75
Outputs:
- update_step: float32 [884736], P('samples')
The draws below stay inside these ranges and needn't reach their ends.
Inputs may be any that keep to these rules, and one draw needn't show every extreme that they name: `spin_configs`: every entry is +1 or -1, and each sample has as many +1 as -1 entries.
All inputs are finite; a program needn't handle non-finite values.
Results may differ from the reference program's by a relative error of at most 0.004.
The reference program's roundings to bfloat16 on the way (of `centered`) count: a program that leaves them out, or rounds other values in their place, can miss the bound.
Values may be sent and summed in bfloat16 or wider, within the bound.
No kernel may reach another device: no remote copies, remote signals or barrier semaphores. Data moves between devices by JAX's collectives and lax.ppermute only.
A program may use at most 128 MiB of HBM per device.

```python
import math
import jax
import jax.numpy as jnp
from jax import lax

SIDE = 16
CH = 64
LAYERS = 24
SITES = 256
NS = 256
P_SIZE = 884736


def draw_spin_configs(key, part):
    sample_keys = jax.random.split(key, NS)

    def one_sample(sample_key):
        ordering = jax.random.permutation(sample_key, SITES)
        return jnp.where(ordering < SITES // 2, 1, -1).astype(jnp.int32)
    return jax.vmap(one_sample)(sample_keys)


def shard_levels(own_key, extent, cuts, low, top_value):
    factor_of, own = 1.0, jax.random.fold_in(own_key, 6)
    for dim, shards_of in cuts:
        draws = jnp.exp(jax.random.uniform(jax.random.fold_in(own, dim), (shards_of,), jnp.float32, low / len(cuts), top_value / len(cuts)))
        factor_of = factor_of * jnp.repeat(draws, extent[dim] // shards_of).reshape([-1 if axis == dim else 1 for axis in range(len(extent))])
    return factor_of


def centred(key, shape, width, most, cuts=(), kind=jnp.bfloat16):
    entries = jax.random.normal(key, shape, jnp.float32) * width
    if len(cuts) > 0:
        entries = shard_levels(key, shape, cuts, -0.22, 0.18) * entries
    return jnp.clip(entries, min=-most, max=most).astype(kind)


def setup_inputs(seed: int = 0) -> dict:
    splits = jax.random.split(jax.random.key(seed), 6)
    spin_configs = draw_spin_configs(jax.random.fold_in(splits[5], 71), 0)
    energy = centred(splits[1], (NS,), 1.0, 6.0, ((0, 256),), jnp.float32)
    embedding = centred(splits[2], (9, CH), 9 ** -0.5, 2.0, (), jnp.float32)
    kernels = centred(splits[3], (LAYERS, 9, CH, CH), (9 * CH) ** -0.5, 0.25, (), jnp.float32)
    readout = centred(splits[4], (CH,), CH ** -0.5, 0.75, (), jnp.float32)
    return dict(spin_configs=spin_configs, energy=energy, embedding=embedding, kernels=kernels, readout=readout)


shift_ratio = 0.05

def shifted_copies(values, lattice_side):
    channels = values.shape[0]
    lattice = values.reshape(channels, lattice_side, lattice_side)
    copies = [jnp.roll(lattice, (row_step, col_step), axis=(1, 2)) for row_step in (1, 0, -1) for col_step in (1, 0, -1)]
    return jnp.stack(copies, 0).reshape(9, channels, lattice_side * lattice_side)

def layer_norm(values):
    deviation = values - lax.optimization_barrier(jnp.mean(values, axis=0, keepdims=True))
    return deviation * lax.rsqrt(lax.optimization_barrier(jnp.mean(deviation * deviation, axis=0, keepdims=True)) + 1e-05)

def block_step(hidden, kernel, lattice_side):
    active = jax.nn.gelu(layer_norm(hidden))
    return hidden + jnp.einsum('kis,kio->os', shifted_copies(active, lattice_side), kernel, precision=lax.Precision.HIGHEST)

def log_amplitude(all_kernels, spin_row, embedding, readout, lattice_side):
    spin_field = spin_row.astype(jnp.float32)[None, :]
    hidden = jnp.einsum('kcs,kcd->ds', shifted_copies(spin_field, lattice_side), embedding[:, None, :], precision=lax.Precision.HIGHEST)
    hidden, unused = lax.scan(lambda carry, kernel: (block_step(carry, kernel, lattice_side), None), hidden, all_kernels)
    return jnp.sum(readout[:, None] * jax.nn.gelu(layer_norm(hidden))) / lattice_side

def solve_coeffs(gram_matrix, energy_all):
    sample_count = gram_matrix.shape[0]
    spread = (energy_all - jnp.mean(energy_all)) / math.sqrt(sample_count)
    diag_term = shift_ratio * jnp.mean(jnp.diagonal(gram_matrix)) + 1e-06
    system = gram_matrix + diag_term * jnp.eye(sample_count, dtype=jnp.float32)
    factor = jnp.linalg.cholesky(system)
    return jax.scipy.linalg.cho_solve((factor, True), spread)

def reference(spin_configs, energy, embedding, kernels, readout):
    gradient = jax.grad(lambda all_kernels, spin_row: log_amplitude(all_kernels, spin_row, embedding, readout, SIDE))

    def group_rows(spin_group):
        return jax.vmap(gradient, in_axes=(None, 0))(kernels, spin_group).reshape(8, P_SIZE)
    logderiv = lax.map(group_rows, spin_configs.reshape(NS // 8, 8, SITES)).reshape(NS, P_SIZE)
    mean_row = lax.optimization_barrier(jnp.mean(logderiv, axis=0))
    centered = ((logderiv - mean_row) / math.sqrt(NS)).astype(jnp.bfloat16)
    gram_matrix = jnp.dot(centered.astype(jnp.float32), centered.T.astype(jnp.float32), preferred_element_type=jnp.float32)
    coeffs = solve_coeffs(gram_matrix, energy)
    blocked = jnp.transpose(centered.reshape(NS, LAYERS, P_SIZE // LAYERS), (1, 0, 2))

    def block_direction(block):
        return jnp.dot(coeffs, block.astype(jnp.float32), precision=lax.Precision.HIGHEST)
    direction = lax.map(block_direction, blocked).reshape(P_SIZE)
    return direction * lax.rsqrt(jnp.mean(direction * direction) + 1e-06)
```

```python
import math

import jax
import jax.numpy as jnp
from jax import lax
from jax.experimental import pallas as pl
from jax.experimental.pallas import tpu as pltpu
from jax.sharding import PartitionSpec as P

SIDE = 16
SITES = 256
CH = 64
LAYERS = 24
NS = 256
TAPS = 9
OWN_ROWS = 27
SEND_SUB = 4
SEND_TILES = 7
SEND_LANES = 128 * SEND_TILES
TOP = 32767.0
LAYER_ROWS = 288
P_SIZE = 884736

SHIFT_RATIO = 0.05
GELU_A = math.sqrt(2.0 / math.pi)
GELU_B = 0.044715

F32 = jnp.float32
BF16 = jnp.bfloat16


def split_two(values):
    high = values.astype(BF16)
    low = (values - high.astype(F32)).astype(BF16)
    return high, low


def matmul(a, b):
    return lax.dot_general(a, b, (((1,), (0,)), ((), ())), preferred_element_type=F32)


def matmul_nt(a, b):
    return lax.dot_general(a, b, (((1,), (1,)), ((), ())), preferred_element_type=F32)


def roll_lanes(values, amount):
    return pltpu.roll(values, amount % SITES, 1)


def shifted_copies(values, column):
    first, last = column == 0, column == SIDE - 1
    right = roll_lanes(values, 1)
    right_up, right_down = roll_lanes(right, -16), roll_lanes(right, 16)
    left = roll_lanes(values, -1)
    left_up, left_down = roll_lanes(left, -16), roll_lanes(left, 16)
    return [
        jnp.where(first, right, right_down),
        roll_lanes(values, 16),
        jnp.where(last, roll_lanes(left, 32), left_down),
        jnp.where(first, right_up, right),
        values,
        jnp.where(last, left_down, left),
        jnp.where(first, roll_lanes(right, -32), right_up),
        roll_lanes(values, -16),
        jnp.where(last, left, left_up),
    ]


def gather_back(parts, column):
    first, last = column == 0, column == SIDE - 1
    rows = [
        roll_lanes(parts[j], -16) + parts[3 + j] + roll_lanes(parts[6 + j], 16) for j in range(3)
    ]
    left = roll_lanes(rows[0], -1)
    right = roll_lanes(rows[2], 1)
    return (
        rows[1]
        + jnp.where(last, roll_lanes(left, 16), left)
        + jnp.where(first, roll_lanes(right, -16), right)
    )


def normalise(hidden):
    deviation = hidden - jnp.mean(hidden, axis=0, keepdims=True)
    scale = lax.rsqrt(jnp.mean(deviation * deviation, axis=0, keepdims=True) + 1e-05)
    return deviation * scale, scale


def activate(n):
    square = n * n
    t = jnp.tanh(GELU_A * (n + GELU_B * (n * square)))
    half = 0.5 * (1.0 + t)
    slope = half + (0.5 * GELU_A) * n * (1.0 - t * t) * (1.0 + (3.0 * GELU_B) * square)
    return n * half, slope


def normalise_back(grad, n, scale):
    return scale * (
        grad
        - jnp.mean(grad, axis=0, keepdims=True)
        - n * jnp.mean(grad * n, axis=0, keepdims=True)
    )


def encode_scale(largest):
    largest = jnp.maximum(largest, 1e-30)
    exponent = jnp.ceil(jnp.log(largest) * (1.0 / math.log(2.0)) + 0.006)
    mantissa = jnp.ceil(largest * jnp.exp2(-exponent) * 512.0 - 256.0)
    return exponent * 256.0 + jnp.clip(mantissa, 0.0, 255.0)


def decode_scale(code):
    exponent = jnp.floor(code * (1.0 / 256.0))
    return jnp.exp2(exponent) * ((code - 256.0 * exponent + 256.0) * (1.0 / 512.0))


def logderiv_kernel(
    spin_ref, embed_ref, readout_ref, kernels_hbm, out_ref,
    weights, u_hi, u_lo, n_all, slope_all, scale_all, rows, pair, sems,
):
    def fetch(layer):
        return pltpu.make_async_copy(kernels_hbm.at[layer], weights.at[layer], sems.at[layer])

    lax.fori_loop(0, LAYERS, lambda i, c: (fetch(i).start(), c)[1], 0)

    column = lax.broadcasted_iota(jnp.int32, (CH, SITES), 1) & (SIDE - 1)
    diagonal = lax.broadcasted_iota(jnp.int32, (CH, CH), 0) == lax.broadcasted_iota(
        jnp.int32, (CH, CH), 1
    )

    def as_column(row):
        return jnp.sum(jnp.where(diagonal, row, 0.0), axis=1, keepdims=True)

    spin = jnp.broadcast_to(spin_ref[...].astype(F32), (8, SITES))
    hidden = jnp.zeros((CH, SITES), F32)
    for k, copy in enumerate(shifted_copies(spin, column[:8])):
        hidden = hidden + as_column(embed_ref[k : k + 1, :]) * copy[0:1, :]

    def forward(layer, hidden):
        fetch(layer).wait()
        n, scale = normalise(hidden)
        u, slope = activate(n)
        n_all[layer] = n
        slope_all[layer] = slope
        scale_all[layer, 0:1, :] = scale
        for half in range(2):
            pair[half] = u[:, 128 * half : 128 * half + 128]
        mixed = jnp.concatenate(
            [
                jnp.concatenate([pair[half, pl.ds(odd, 32, stride=2), :] for half in range(2)], 1)
                for odd in range(2)
            ],
            0,
        )
        for k, copy in enumerate(shifted_copies(mixed, column)):
            high, low = split_two(copy)
            for odd in range(2):
                place = pl.ds(LAYER_ROWS * odd + 32 * k, 32)
                u_hi[layer, place, :] = high[32 * odd : 32 * odd + 32]
                u_lo[layer, place, :] = low[32 * odd : 32 * odd + 32]
        taps = jnp.concatenate(
            [weights[layer, pl.ds(odd, LAYER_ROWS, stride=2), :] for odd in range(2)], 0
        )
        w_hi, w_lo = split_two(taps.T)
        both = matmul(jnp.concatenate([w_hi, w_lo], 0), u_hi[layer])
        rest = matmul(w_hi, u_lo[layer])
        return hidden + (both[:CH] + (both[CH:] + rest))

    hidden = lax.fori_loop(0, LAYERS, forward, hidden)

    n, scale = normalise(hidden)
    _, slope = activate(n)
    grad = normalise_back((as_column(readout_ref[...]) * (1.0 / SIDE)) * slope, n, scale)
    zeros = jnp.zeros((CH, SITES), BF16)

    def backward(step, grad):
        layer = LAYERS - 1 - step
        high, low = split_two(grad)
        wide = jnp.concatenate(split_two(weights[layer]), 1)
        taps = matmul(
            jnp.concatenate([wide, wide], 1), jnp.concatenate([high, high, low, low], 0)
        )
        even = jnp.concatenate([high, zeros, low, zeros], 0)
        odd = jnp.concatenate([zeros, high, zeros, low], 0)
        top, bottom = pl.ds(0, LAYER_ROWS), pl.ds(LAYER_ROWS, LAYER_ROWS)
        main = matmul_nt(u_hi[layer, top, :], even) + matmul_nt(u_hi[layer, bottom, :], odd)
        rest = matmul_nt(u_lo[layer, top, :], even[:128]) + matmul_nt(u_lo[layer, bottom, :], odd[:128])
        entries = main[:, :128] + (main[:, 128:] + rest)
        rows[pl.ds(pl.multiple_of(layer * LAYER_ROWS, 8), LAYER_ROWS), :] = entries
        back = gather_back([taps[CH * k : CH * k + CH] for k in range(TAPS)], column)
        return grad + normalise_back(back * slope_all[layer], n_all[layer], scale_all[layer, 0:1, :])

    lax.fori_loop(0, LAYERS, backward, grad)

    spare = lax.broadcasted_iota(jnp.int32, (SEND_SUB, 128), 0) == SEND_SUB - 1

    def place_rows(block, carry):
        source = pl.multiple_of(block * (8 * OWN_ROWS), 8)
        for j in range(8):
            tiles = [
                rows[pl.ds(source + (OWN_ROWS * j + SEND_SUB * t), SEND_SUB), :]
                for t in range(SEND_TILES)
            ]
            tiles[-1] = jnp.where(spare, 0.0, tiles[-1])
            largest = jnp.abs(tiles[0])
            for tile in tiles[1:]:
                largest = jnp.maximum(largest, jnp.abs(tile))
            code = encode_scale(jnp.max(largest, axis=0, keepdims=True))
            factor = TOP / decode_scale(code)
            coded = [jnp.round(tile * factor) for tile in tiles]
            coded[-1] = jnp.where(spare, code, coded[-1])
            out_ref[block * 8 + j] = jnp.concatenate(coded, 1).astype(jnp.int32).astype(jnp.int16)
        return carry

    lax.fori_loop(0, NS // 8, place_rows, 0)


def logderiv_rows(spin, embedding, kernels, readout):
    vmem = pl.BlockSpec(memory_space=pltpu.VMEM)
    hbm = pl.BlockSpec(memory_space=pl.ANY)
    return pl.pallas_call(
        logderiv_kernel,
        out_shape=jax.ShapeDtypeStruct((NS, SEND_SUB, SEND_LANES), jnp.int16),
        in_specs=[vmem, vmem, vmem, hbm],
        out_specs=vmem,
        scratch_shapes=[
            pltpu.VMEM((LAYERS, TAPS * CH, CH), F32),
            pltpu.VMEM((LAYERS, TAPS * CH, SITES), BF16),
            pltpu.VMEM((LAYERS, TAPS * CH, SITES), BF16),
            pltpu.VMEM((LAYERS, CH, SITES), F32),
            pltpu.VMEM((LAYERS, CH, SITES), F32),
            pltpu.VMEM((LAYERS, 8, SITES), F32),
            pltpu.VMEM((LAYERS * LAYER_ROWS + 8, 128), F32),
            pltpu.VMEM((2, CH, 128), F32),
            pltpu.SemaphoreType.DMA((LAYERS,)),
        ],
        compiler_params=pltpu.CompilerParams(vmem_limit_bytes=60 << 20),
        name="logderiv",
    )(spin, embedding, readout, kernels.reshape(LAYERS, TAPS * CH, CH))


def gram_kernel(x_ref, centered_ref, gram_ref, values):
    lower = lax.broadcasted_iota(jnp.int32, (2 * SEND_SUB, 128), 0) < SEND_SUB

    def widen(block, carry):
        for j in range(4):
            first = block * 8 + 2 * j
            both = jnp.concatenate([x_ref[first + i].astype(jnp.int32).astype(F32) for i in range(2)], 0)
            code = both[:, SEND_LANES - 128 :]
            code = jnp.where(lower, code[SEND_SUB - 1 : SEND_SUB], code[2 * SEND_SUB - 1 : 2 * SEND_SUB])
            scale = decode_scale(code) * (1.0 / TOP)
            place = pl.ds(pl.multiple_of(first * SEND_SUB, 8), 2 * SEND_SUB)
            for t in range(SEND_TILES):
                values[t, place, :] = both[:, 128 * t : 128 * t + 128] * scale
        return carry

    lax.fori_loop(0, NS // 8, widen, 0)
    total = jnp.zeros((NS, NS), F32)
    held = None
    for r in range(OWN_ROWS):
        entries = values[r // SEND_SUB, pl.ds(r % SEND_SUB, NS, stride=SEND_SUB), :]
        mean = jnp.sum(entries, axis=0, keepdims=True) * (1.0 / NS)
        centered = ((entries - mean) * (1.0 / math.sqrt(NS))).astype(BF16)
        centered_ref[:, 128 * r : 128 * r + 128] = centered
        if held is None and r + 1 < OWN_ROWS:
            held = centered
        elif held is None:
            total = total + matmul_nt(centered, centered)
        else:
            wide = jnp.concatenate([held, centered], 1)
            total = total + matmul_nt(wide, wide)
            held = None
    gram_ref[...] = total


def partial_gram(x):
    vmem = pl.BlockSpec(memory_space=pltpu.VMEM)
    return pl.pallas_call(
        gram_kernel,
        out_shape=(
            jax.ShapeDtypeStruct((NS, OWN_ROWS * 128), BF16),
            jax.ShapeDtypeStruct((NS, NS), F32),
        ),
        in_specs=[vmem],
        out_specs=(vmem, vmem),
        scratch_shapes=[pltpu.VMEM((SEND_TILES, NS * SEND_SUB, 128), F32)],
        compiler_params=pltpu.CompilerParams(vmem_limit_bytes=40 << 20),
        name="partial_gram",
    )(x)


def direction_kernel(table_ref, centered_ref, out_ref, system):
    diagonal = lax.broadcasted_iota(jnp.int32, (NS, NS), 0) == lax.broadcasted_iota(
        jnp.int32, (NS, NS), 1
    )

    def total(values):
        return jnp.sum(values, axis=1, keepdims=True)

    def as_row(values):
        return jnp.sum(jnp.where(diagonal, values, 0.0), axis=0, keepdims=True)

    gram = table_ref[:, :NS]
    energy = as_row(table_ref[:, NS : NS + 1])
    spread = (energy - total(energy) * (1.0 / NS)) * (1.0 / math.sqrt(NS))
    diag_term = SHIFT_RATIO * (total(as_row(gram)) * (1.0 / NS)) + 1e-06
    system[...] = gram + jnp.where(diagonal, diag_term, 0.0)
    tiny = 1e-37

    def iterate(state):
        count, x, r, p, rr = state
        for _ in range(4):
            q = as_row(total(system[...] * p))
            alpha = rr / jnp.maximum(total(p * q), tiny)
            x = x + alpha * p
            r = r - alpha * q
            latest = total(r * r)
            p = r + (latest / jnp.maximum(rr, tiny)) * p
            rr = latest
        return count + 1, x, r, p, rr

    start = total(spread * spread)
    goal = start * 1e-13
    _, coeffs, _, _, _ = lax.while_loop(
        lambda state: (state[0] < 512) & ((state[4] - goal)[0, 0] > 0.0),
        iterate,
        (jnp.int32(0), jnp.zeros((1, NS), F32), spread, spread, start),
    )
    square_total = total(coeffs * as_row(total(table_ref[:, :NS] * coeffs)))
    high = coeffs.astype(BF16).astype(F32)
    middle = (coeffs - high).astype(BF16).astype(F32)
    low = coeffs - high - middle
    line = lax.broadcasted_iota(jnp.int32, (16, NS), 0)
    parts = jnp.where(line == 0, high, jnp.where(line == 1, middle, jnp.where(line == 2, low, 0.0)))
    own = jnp.sum(matmul(parts.astype(BF16), centered_ref[...]), axis=0, keepdims=True)
    out_ref[...] = own * lax.rsqrt(square_total * (1.0 / P_SIZE) + 1e-06)


def direction(table, centered):
    vmem = pl.BlockSpec(memory_space=pltpu.VMEM)
    return pl.pallas_call(
        direction_kernel,
        out_shape=jax.ShapeDtypeStruct((1, OWN_ROWS * 128), F32),
        in_specs=[vmem, vmem],
        out_specs=vmem,
        scratch_shapes=[pltpu.VMEM((NS, NS), F32)],
        compiler_params=pltpu.CompilerParams(vmem_limit_bytes=40 << 20),
        name="direction",
    )(table, centered)


def exchange(blocks):
    return lax.all_to_all(blocks, "samples", split_axis=0, concat_axis=0, tiled=True)


def per_device(spin_configs, energy, embedding, kernels, readout):
    own = logderiv_rows(spin_configs, embedding, kernels, readout.reshape(1, CH))
    centered, part = partial_gram(exchange(own))
    gram_row = jnp.sum(exchange(part.reshape(NS, 1, NS)), axis=0)
    line = jnp.concatenate([gram_row, jnp.broadcast_to(energy[:, None], (1, 128))], 1)
    table = exchange(jnp.broadcast_to(line[None], (NS, 1, NS + 128))).reshape(NS, NS + 128)
    return direction(table, centered).reshape(-1)


def solution(mesh):
    return jax.shard_map(
        per_device,
        mesh=mesh,
        in_specs=(P("samples", None), P("samples"), P(), P(), P()),
        out_specs=P("samples"),
        check_vma=False,
    )
```

```python
import math

import jax
import jax.numpy as jnp
from jax import lax
from jax.experimental import pallas as pl
from jax.experimental.pallas import tpu as pltpu
from jax.sharding import PartitionSpec as P

SIDE = 16
SITES = 256
CH = 64
LAYERS = 24
NS = 256
TAPS = 9
OWN_ROWS = 27
SEND_SUB = 4
STEP_CHUNKS = 11
SEND_TILES = 7
SEND_LANES = 128 * SEND_TILES
TOP = 32767.0
LAYER_ROWS = 288
P_SIZE = 884736

SHIFT_RATIO = 0.05
GELU_A = math.sqrt(2.0 / math.pi)
GELU_B = 0.044715

F32 = jnp.float32
BF16 = jnp.bfloat16


def split_two(values):
    high = values.astype(BF16)
    low = (values - high.astype(F32)).astype(BF16)
    return high, low


def matmul(a, b):
    return lax.dot_general(a, b, (((1,), (0,)), ((), ())), preferred_element_type=F32)


def matmul_nt(a, b):
    return lax.dot_general(a, b, (((1,), (1,)), ((), ())), preferred_element_type=F32)


def roll_lanes(values, amount):
    return pltpu.roll(values, amount % SITES, 1)


def shifted_copies(values, column):
    first, last = column == 0, column == SIDE - 1
    right = roll_lanes(values, 1)
    right_up, right_down = roll_lanes(right, -16), roll_lanes(right, 16)
    left = roll_lanes(values, -1)
    left_up, left_down = roll_lanes(left, -16), roll_lanes(left, 16)
    return [
        jnp.where(first, right, right_down),
        roll_lanes(values, 16),
        jnp.where(last, roll_lanes(left, 32), left_down),
        jnp.where(first, right_up, right),
        values,
        jnp.where(last, left_down, left),
        jnp.where(first, roll_lanes(right, -32), right_up),
        roll_lanes(values, -16),
        jnp.where(last, left, left_up),
    ]


def gather_back(parts, column):
    first, last = column == 0, column == SIDE - 1
    rows = [
        roll_lanes(parts[j], -16) + parts[3 + j] + roll_lanes(parts[6 + j], 16) for j in range(3)
    ]
    left = roll_lanes(rows[0], -1)
    right = roll_lanes(rows[2], 1)
    return (
        rows[1]
        + jnp.where(last, roll_lanes(left, 16), left)
        + jnp.where(first, roll_lanes(right, -16), right)
    )


def normalise(hidden):
    deviation = hidden - jnp.mean(hidden, axis=0, keepdims=True)
    scale = lax.rsqrt(jnp.mean(deviation * deviation, axis=0, keepdims=True) + 1e-05)
    return deviation * scale, scale


def activate(n):
    square = n * n
    t = jnp.tanh(GELU_A * (n + GELU_B * (n * square)))
    half = 0.5 * (1.0 + t)
    slope = half + (0.5 * GELU_A) * n * (1.0 - t * t) * (1.0 + (3.0 * GELU_B) * square)
    return n * half, slope


def normalise_back(grad, n, scale):
    return scale * (
        grad
        - jnp.mean(grad, axis=0, keepdims=True)
        - n * jnp.mean(grad * n, axis=0, keepdims=True)
    )


def encode_scale(largest):
    largest = jnp.maximum(largest, 1e-30)
    exponent = jnp.ceil(jnp.log(largest) * (1.0 / math.log(2.0)) + 0.006)
    mantissa = jnp.ceil(largest * jnp.exp2(-exponent) * 512.0 - 256.0)
    return exponent * 256.0 + jnp.clip(mantissa, 0.0, 255.0)


def decode_scale(code):
    exponent = jnp.floor(code * (1.0 / 256.0))
    return jnp.exp2(exponent) * ((code - 256.0 * exponent + 256.0) * (1.0 / 512.0))


def logderiv_kernel(
    spin_ref, embed_ref, readout_ref, kernels_hbm, out_ref,
    weights, u_hi, u_lo, n_all, slope_all, scale_all, rows, pair, sems,
):
    def fetch(layer):
        return pltpu.make_async_copy(kernels_hbm.at[layer], weights.at[layer], sems.at[layer])

    lax.fori_loop(0, LAYERS, lambda i, c: (fetch(i).start(), c)[1], 0)

    column = lax.broadcasted_iota(jnp.int32, (CH, SITES), 1) & (SIDE - 1)
    diagonal = lax.broadcasted_iota(jnp.int32, (CH, CH), 0) == lax.broadcasted_iota(
        jnp.int32, (CH, CH), 1
    )

    unit = jnp.where(diagonal, 1.0, 0.0).astype(BF16)

    def as_column(row):
        return jnp.sum(jnp.where(diagonal, row, 0.0), axis=1, keepdims=True)

    spin = jnp.broadcast_to(spin_ref[...].astype(F32), (8, SITES))
    hidden = jnp.zeros((CH, SITES), F32)
    for k, copy in enumerate(shifted_copies(spin, column[:8])):
        hidden = hidden + as_column(embed_ref[k : k + 1, :]) * copy[0:1, :]

    def forward(layer, hidden):
        fetch(layer).wait()
        n, scale = normalise(hidden)
        u, slope = activate(n)
        n_all[layer] = n
        slope_all[layer] = slope
        scale_all[layer, 0:1, :] = scale
        for half in range(2):
            pair[half] = u[:, 128 * half : 128 * half + 128]
        mixed = jnp.concatenate(
            [
                jnp.concatenate([pair[half, pl.ds(odd, 32, stride=2), :] for half in range(2)], 1)
                for odd in range(2)
            ],
            0,
        )
        for store, part in zip((u_hi, u_lo), split_two(mixed)):
            for k, copy in enumerate(shifted_copies(part, column)):
                for odd in range(2):
                    place = pl.ds(LAYER_ROWS * odd + 32 * k, 32)
                    store[layer, place, :] = copy[32 * odd : 32 * odd + 32]
        taps = jnp.concatenate(
            [weights[layer, pl.ds(odd, LAYER_ROWS, stride=2), :] for odd in range(2)], 0
        )
        w_hi, w_lo = [matmul_nt(unit, part).astype(BF16) for part in split_two(taps)]
        both = matmul(jnp.concatenate([w_hi, w_lo], 0), u_hi[layer])
        rest = matmul(w_hi, u_lo[layer])
        return hidden + (both[:CH] + (both[CH:] + rest))

    hidden = lax.fori_loop(0, LAYERS, forward, hidden)

    n, scale = normalise(hidden)
    _, slope = activate(n)
    grad = normalise_back((as_column(readout_ref[...]) * (1.0 / SIDE)) * slope, n, scale)
    zeros = jnp.zeros((CH, SITES), BF16)

    spare = lax.broadcasted_iota(jnp.int32, (SEND_SUB, 128), 0) == SEND_SUB - 1

    def place_chunk(chunk):
        tiles = [rows[pl.ds(chunk * OWN_ROWS + SEND_SUB * t, SEND_SUB), :] for t in range(SEND_TILES)]
        tiles[-1] = jnp.where(spare, 0.0, tiles[-1])
        largest = jnp.abs(tiles[0])
        for tile in tiles[1:]:
            largest = jnp.maximum(largest, jnp.abs(tile))
        code = encode_scale(jnp.max(largest, axis=0, keepdims=True))
        factor = TOP / decode_scale(code)
        coded = [jnp.round(tile * factor) for tile in tiles]
        coded[-1] = jnp.where(spare, code, coded[-1])
        out_ref[chunk] = jnp.concatenate(coded, 1).astype(jnp.int32).astype(jnp.int16)

    def backward(step, grad):
        layer = LAYERS - 1 - step
        first = (LAYER_ROWS * (layer + 1) + OWN_ROWS - 1) // OWN_ROWS
        for j in range(STEP_CHUNKS):
            place_chunk(jnp.minimum(first + j, NS - 1))
        high, low = split_two(grad)
        wide = jnp.concatenate(split_two(weights[layer]), 1)
        taps = matmul(
            jnp.concatenate([wide, wide], 1), jnp.concatenate([high, high, low, low], 0)
        )
        even = jnp.concatenate([high, zeros, low, zeros], 0)
        odd = jnp.concatenate([zeros, high, zeros, low], 0)
        top, bottom = pl.ds(0, LAYER_ROWS), pl.ds(LAYER_ROWS, LAYER_ROWS)
        main = matmul_nt(u_hi[layer, top, :], even) + matmul_nt(u_hi[layer, bottom, :], odd)
        rest = matmul_nt(u_lo[layer, top, :], even[:128]) + matmul_nt(u_lo[layer, bottom, :], odd[:128])
        entries = main[:, :128] + (main[:, 128:] + rest)
        rows[pl.ds(pl.multiple_of(layer * LAYER_ROWS, 8), LAYER_ROWS), :] = entries
        back = gather_back([taps[CH * k : CH * k + CH] for k in range(TAPS)], column)
        return grad + normalise_back(back * slope_all[layer], n_all[layer], scale_all[layer, 0:1, :])

    lax.fori_loop(0, LAYERS, backward, grad)

    for chunk in range(STEP_CHUNKS):
        place_chunk(chunk)


def logderiv_rows(spin, embedding, kernels, readout):
    vmem = pl.BlockSpec(memory_space=pltpu.VMEM)
    hbm = pl.BlockSpec(memory_space=pl.ANY)
    return pl.pallas_call(
        logderiv_kernel,
        out_shape=jax.ShapeDtypeStruct((NS, SEND_SUB, SEND_LANES), jnp.int16),
        in_specs=[vmem, vmem, vmem, hbm],
        out_specs=vmem,
        scratch_shapes=[
            pltpu.VMEM((LAYERS, TAPS * CH, CH), F32),
            pltpu.VMEM((LAYERS, TAPS * CH, SITES), BF16),
            pltpu.VMEM((LAYERS, TAPS * CH, SITES), BF16),
            pltpu.VMEM((LAYERS, CH, SITES), F32),
            pltpu.VMEM((LAYERS, CH, SITES), F32),
            pltpu.VMEM((LAYERS, 8, SITES), F32),
            pltpu.VMEM((LAYERS * LAYER_ROWS + 8, 128), F32),
            pltpu.VMEM((2, CH, 128), F32),
            pltpu.SemaphoreType.DMA((LAYERS,)),
        ],
        compiler_params=pltpu.CompilerParams(vmem_limit_bytes=60 << 20),
        name="logderiv",
    )(spin, embedding, readout, kernels.reshape(LAYERS, TAPS * CH, CH))


def gram_kernel(x_ref, centered_ref, gram_ref, values):
    lower = lax.broadcasted_iota(jnp.int32, (2 * SEND_SUB, 128), 0) < SEND_SUB

    def widen(block, carry):
        for j in range(4):
            first = block * 8 + 2 * j
            both = jnp.concatenate([x_ref[first + i].astype(jnp.int32).astype(F32) for i in range(2)], 0)
            code = both[:, SEND_LANES - 128 :]
            code = jnp.where(lower, code[SEND_SUB - 1 : SEND_SUB], code[2 * SEND_SUB - 1 : 2 * SEND_SUB])
            scale = decode_scale(code) * (1.0 / TOP)
            place = pl.ds(pl.multiple_of(first * SEND_SUB, 8), 2 * SEND_SUB)
            for t in range(SEND_TILES):
                values[t, place, :] = both[:, 128 * t : 128 * t + 128] * scale
        return carry

    lax.fori_loop(0, NS // 8, widen, 0)
    total = jnp.zeros((NS, NS), F32)
    held = None
    for r in range(OWN_ROWS):
        entries = values[r // SEND_SUB, pl.ds(r % SEND_SUB, NS, stride=SEND_SUB), :]
        mean = jnp.sum(entries, axis=0, keepdims=True) * (1.0 / NS)
        centered = ((entries - mean) * (1.0 / math.sqrt(NS))).astype(BF16)
        centered_ref[:, 128 * r : 128 * r + 128] = centered
        if held is None and r + 1 < OWN_ROWS:
            held = centered
        elif held is None:
            total = total + matmul_nt(centered, centered)
        else:
            wide = jnp.concatenate([held, centered], 1)
            total = total + matmul_nt(wide, wide)
            held = None
    gram_ref[:, 0, :] = total


def partial_gram(x):
    vmem = pl.BlockSpec(memory_space=pltpu.VMEM)
    return pl.pallas_call(
        gram_kernel,
        out_shape=(
            jax.ShapeDtypeStruct((NS, OWN_ROWS * 128), BF16),
            jax.ShapeDtypeStruct((NS, 1, NS), F32),
        ),
        in_specs=[vmem],
        out_specs=(vmem, vmem),
        scratch_shapes=[pltpu.VMEM((SEND_TILES, NS * SEND_SUB, 128), F32)],
        compiler_params=pltpu.CompilerParams(vmem_limit_bytes=40 << 20),
        name="partial_gram",
    )(x)


def direction_kernel(table_ref, centered_ref, out_ref, system, r_col, s_col):
    diagonal = lax.broadcasted_iota(jnp.int32, (NS, NS), 0) == lax.broadcasted_iota(
        jnp.int32, (NS, NS), 1
    )

    def total(values):
        return jnp.sum(values, axis=1, keepdims=True)

    def as_column(values):
        return total(jnp.where(diagonal, values, 0.0))

    def as_row(values):
        return jnp.sum(jnp.where(diagonal, values, 0.0), axis=0, keepdims=True)

    gram = table_ref[:, :NS]
    energy = as_row(table_ref[:, NS : NS + 1])
    spread = (energy - total(energy) * (1.0 / NS)) * (1.0 / math.sqrt(NS))
    diag_term = SHIFT_RATIO * (total(as_row(gram)) * (1.0 / NS)) + 1e-06
    system[...] = gram + jnp.where(diagonal, diag_term, 0.0)
    tiny = 1e-37

    def twice(values):
        return jnp.concatenate([values, values], 1)

    def iterate(state):
        count, x, r, p, s, last, alpha, _ = state
        for _ in range(4):
            w_col = total(system[...] * r)
            r_all = r_col[...]
            norm = jnp.sum(r_all * r_all, axis=0, keepdims=True)
            delta = jnp.sum(r_all * w_col, axis=0, keepdims=True)
            beta = norm / jnp.maximum(last, tiny)
            alpha = norm / jnp.maximum(delta - beta * norm / jnp.maximum(alpha, tiny), tiny)
            last = norm
            s_all = w_col + beta * s_col[...]
            s_col[...] = s_all
            r_col[...] = r_all - alpha * s_all
            p = r + twice(beta) * p
            s = as_row(w_col) + twice(beta) * s
            x = x + twice(alpha) * p
            r = r - twice(alpha) * s
        return count + 1, x, r, p, s, last, alpha, norm

    spread_col = jnp.broadcast_to(as_column(spread), (NS, 128))
    r_col[...] = spread_col
    s_col[...] = jnp.zeros((NS, 128), F32)
    start = jnp.sum(spread_col * spread_col, axis=0, keepdims=True)
    goal = start * 1e-13
    zero = jnp.zeros((1, NS), F32)
    _, coeffs, _, _, _, _, _, _ = lax.while_loop(
        lambda state: (state[0] < 512) & ((state[7] - goal)[0, 0] > 0.0),
        iterate,
        (jnp.int32(0), zero, spread, zero, zero, jnp.full((1, 128), 1e30, F32), jnp.ones((1, 128), F32), start),
    )
    square_total = total(coeffs * as_row(total(table_ref[:, :NS] * coeffs)))
    high = coeffs.astype(BF16).astype(F32)
    middle = (coeffs - high).astype(BF16).astype(F32)
    low = coeffs - high - middle
    line = lax.broadcasted_iota(jnp.int32, (16, NS), 0)
    parts = jnp.where(line == 0, high, jnp.where(line == 1, middle, jnp.where(line == 2, low, 0.0)))
    own = jnp.sum(matmul(parts.astype(BF16), centered_ref[...]), axis=0, keepdims=True)
    out_ref[...] = (own * lax.rsqrt(square_total * (1.0 / P_SIZE) + 1e-06))[0]


def direction(table, centered):
    vmem = pl.BlockSpec(memory_space=pltpu.VMEM)
    return pl.pallas_call(
        direction_kernel,
        out_shape=jax.ShapeDtypeStruct((OWN_ROWS * 128,), F32),
        in_specs=[vmem, vmem],
        out_specs=vmem,
        scratch_shapes=[pltpu.VMEM((NS, NS), F32), pltpu.VMEM((NS, 128), F32), pltpu.VMEM((NS, 128), F32)],
        compiler_params=pltpu.CompilerParams(vmem_limit_bytes=40 << 20),
        name="direction",
    )(table, centered)


def exchange(blocks):
    return lax.all_to_all(blocks, "samples", split_axis=0, concat_axis=0, tiled=True)


def per_device(spin_configs, energy, embedding, kernels, readout):
    own = logderiv_rows(spin_configs, embedding, kernels, readout.reshape(1, CH))
    centered, part = partial_gram(exchange(own))
    gram_row = jnp.sum(exchange(part), axis=0)
    line = jnp.concatenate([gram_row, jnp.broadcast_to(energy[:, None], (1, 128))], 1)
    table = exchange(jnp.broadcast_to(line[None], (NS, 1, NS + 128))).reshape(NS, NS + 128)
    return direction(table, centered)


def solution(mesh):
    return jax.shard_map(
        per_device,
        mesh=mesh,
        in_specs=(P("samples", None), P("samples"), P(), P(), P()),
        out_specs=P("samples"),
        check_vma=False,
    )
```

```python
import math

import jax
import jax.numpy as jnp
from jax import lax
from jax.experimental import pallas as pl
from jax.experimental.pallas import tpu as pltpu
from jax.sharding import PartitionSpec as P

SIDE = 16
SITES = 256
HALF = 128
CH = 64
LAYERS = 24
NS = 256
TAPS = 9
STEPS = (1, 0, -1)
WIDE = 192
OWN_ROWS = 27
SEND_SUB = 4
STEP_CHUNKS = 11
SEND_TILES = 7
SEND_LANES = 128 * SEND_TILES
TOP = 32767.0
LAYER_ROWS = 288
P_SIZE = 884736

SHIFT_RATIO = 0.05
GELU_A = math.sqrt(2.0 / math.pi)
GELU_B = 0.044715

F32 = jnp.float32
BF16 = jnp.bfloat16


def split_two(values):
    high = values.astype(BF16)
    low = (values - high.astype(F32)).astype(BF16)
    return high, low


def matmul(a, b):
    return lax.dot_general(a, b, (((1,), (0,)), ((), ())), preferred_element_type=F32)


def matmul_nt(a, b):
    return lax.dot_general(a, b, (((1,), (1,)), ((), ())), preferred_element_type=F32)


def roll_lanes(values, amount):
    return pltpu.roll(values, amount % HALF, 1)


def halves(values):
    return values[:, :HALF], values[:, HALF:]


def join(even, odd):
    return jnp.concatenate([even, odd], 1)


def column_before(odd, place):
    return jnp.where(place == 0, roll_lanes(odd, -7), roll_lanes(odd, 1))


def column_after(even, place):
    return jnp.where(place == 7, roll_lanes(even, 7), roll_lanes(even, -1))


def column_roll(values, step, place):
    even, odd = halves(values)
    if step == 1:
        return join(column_before(odd, place), even)
    if step == -1:
        return join(odd, column_after(even, place))
    return values


def row_roll(values, step):
    if step == 0:
        return values
    even, odd = halves(values)
    return join(roll_lanes(even, 8 * step), roll_lanes(odd, 8 * step))


def normalise(hidden):
    deviation = hidden - jnp.mean(hidden, axis=0, keepdims=True)
    scale = lax.rsqrt(jnp.mean(deviation * deviation, axis=0, keepdims=True) + 1e-05)
    return deviation * scale, scale


def activate(n):
    square = n * n
    t = jnp.tanh(GELU_A * (n + GELU_B * (n * square)))
    half = 0.5 * (1.0 + t)
    slope = half + (0.5 * GELU_A) * n * (1.0 - t * t) * (1.0 + (3.0 * GELU_B) * square)
    return n * half, slope


def normalise_back(grad, n, scale):
    return scale * (
        grad
        - jnp.mean(grad, axis=0, keepdims=True)
        - n * jnp.mean(grad * n, axis=0, keepdims=True)
    )


def encode_scale(largest):
    largest = jnp.maximum(largest, 1e-30)
    exponent = jnp.ceil(jnp.log(largest) * (1.0 / math.log(2.0)) + 0.006)
    mantissa = jnp.ceil(largest * jnp.exp2(-exponent) * 512.0 - 256.0)
    return exponent * 256.0 + jnp.clip(mantissa, 0.0, 255.0)


def decode_scale(code):
    exponent = jnp.floor(code * (1.0 / 256.0))
    return jnp.exp2(exponent) * ((code - 256.0 * exponent + 256.0) * (1.0 / 512.0))


def logderiv_kernel(
    spin_ref, embed_ref, readout_ref, kernels_hbm, out_ref,
    weights, u_hi, u_lo, n_all, slope_all, scale_all, rows, pair, sems,
):
    def fetch(layer):
        return pltpu.make_async_copy(kernels_hbm.at[layer], weights.at[layer], sems.at[layer])

    lax.fori_loop(0, LAYERS, lambda i, c: (fetch(i).start(), c)[1], 0)

    place = lax.broadcasted_iota(jnp.int32, (CH, HALF), 1) & 7
    diagonal = lax.broadcasted_iota(jnp.int32, (CH, CH), 0) == lax.broadcasted_iota(
        jnp.int32, (CH, CH), 1
    )

    def as_column(row):
        return jnp.sum(jnp.where(diagonal, row, 0.0), axis=1, keepdims=True)

    source = lax.broadcasted_iota(jnp.int32, (SITES, SITES), 0)
    target = lax.broadcasted_iota(jnp.int32, (SITES, SITES), 1)
    wanted = ((target & 127) >> 3) * SIDE + 2 * (target & 7) + (target >> 7)
    order = jnp.where(source == wanted, 1.0, 0.0).astype(BF16)
    spin = matmul(jnp.broadcast_to(spin_ref[...].astype(F32), (16, SITES)).astype(BF16), order)[:8]
    hidden = jnp.zeros((CH, SITES), F32)
    for k in range(TAPS):
        copy = row_roll(column_roll(spin, STEPS[k % 3], place[:8]), STEPS[k // 3])
        hidden = hidden + as_column(embed_ref[k : k + 1, :]) * copy[0:1, :]

    def forward(layer, hidden):
        fetch(layer).wait()
        n, scale = normalise(hidden)
        u, slope = activate(n)
        n_all[layer] = n
        slope_all[layer] = slope
        scale_all[layer, 0:1, :] = scale
        for half in range(2):
            pair[half] = u[:, 128 * half : 128 * half + 128]
        mixed = jnp.concatenate(
            [
                jnp.concatenate([pair[half, pl.ds(odd, 32, stride=2), :] for half in range(2)], 1)
                for odd in range(2)
            ],
            0,
        )
        for store, part in zip((u_hi, u_lo), split_two(mixed)):
            for i, step in enumerate(STEPS):
                store[layer, pl.ds(CH * i, CH), :] = row_roll(part, step)
        groups = [
            split_two(
                jnp.concatenate(
                    [
                        weights[layer, pl.ds(CH * (3 * i + j) + odd, 32, stride=2), :]
                        for i in range(3)
                        for odd in range(2)
                    ],
                    0,
                )
            )
            for j in range(3)
        ]
        w_hi, w_lo = [
            jnp.concatenate([group[i].T for group in groups], 0)
            for i in range(2)
        ]
        sums = matmul(w_hi, u_hi[layer]) + (matmul(w_hi, u_lo[layer]) + matmul(w_lo, u_hi[layer]))
        moved = [column_roll(sums[CH * i : CH * i + CH], step, place) for i, step in enumerate(STEPS)]
        return hidden + (moved[0] + moved[1] + moved[2])

    hidden = lax.fori_loop(0, LAYERS, forward, hidden)

    n, scale = normalise(hidden)
    _, slope = activate(n)
    grad = normalise_back((as_column(readout_ref[...]) * (1.0 / SIDE)) * slope, n, scale)
    left = lax.broadcasted_iota(jnp.int32, (32, 128), 1) < CH

    spare = lax.broadcasted_iota(jnp.int32, (SEND_SUB, 128), 0) == SEND_SUB - 1

    def place_chunk(chunk):
        tiles = [rows[pl.ds(chunk * OWN_ROWS + SEND_SUB * t, SEND_SUB), :] for t in range(SEND_TILES)]
        tiles[-1] = jnp.where(spare, 0.0, tiles[-1])
        largest = jnp.abs(tiles[0])
        for tile in tiles[1:]:
            largest = jnp.maximum(largest, jnp.abs(tile))
        code = encode_scale(jnp.max(largest, axis=0, keepdims=True))
        factor = TOP / decode_scale(code)
        coded = [jnp.round(tile * factor) for tile in tiles]
        coded[-1] = jnp.where(spare, code, coded[-1])
        out_ref[chunk] = jnp.concatenate(coded, 1).astype(jnp.int32).astype(jnp.int16)

    def backward(step, grad):
        layer = LAYERS - 1 - step
        first = (LAYER_ROWS * (layer + 1) + OWN_ROWS - 1) // OWN_ROWS
        for j in range(STEP_CHUNKS):
            place_chunk(jnp.minimum(first + j, NS - 1))
        high, low = split_two(grad)
        g_hi, g_lo = [
            jnp.concatenate([column_roll(part, -step, place) for step in STEPS], 0)
            for part in (high, low)
        ]
        w_hi, w_lo = [
            jnp.concatenate(
                [
                    jnp.concatenate([part[CH * (3 * i + j) : CH * (3 * i + j) + CH] for j in range(3)], 1)
                    for i in range(3)
                ],
                0,
            )
            for part in split_two(weights[layer])
        ]
        sums = matmul(w_hi, g_hi) + (matmul(w_hi, g_lo) + matmul(w_lo, g_hi))
        x_hi, x_lo = [jnp.concatenate([part, part[128:]], 0) for part in (g_hi, g_lo)]
        both = matmul_nt(jnp.concatenate([u_hi[layer], u_lo[layer]], 0), x_hi)
        products = both[:WIDE] + (both[WIDE:] + matmul_nt(u_hi[layer], x_lo))
        for i in range(3):
            even, odd = products[CH * i : CH * i + 32], products[CH * i + 32 : CH * i + CH]
            packed = (
                jnp.where(left, even[:, :128], pltpu.roll(odd[:, :128], CH, 1)),
                jnp.where(left, pltpu.roll(even[:, :128], CH, 1), odd[:, :128]),
                jnp.where(left, even[:, 128:], odd[:, 128:]),
            )
            for j in range(3):
                target_rows = pl.multiple_of(layer * LAYER_ROWS + 32 * (3 * i + j), 8)
                rows[pl.ds(target_rows, 32), :] = packed[j]
        turned = [row_roll(sums[CH * i : CH * i + CH], -step) for i, step in enumerate(STEPS)]
        back = turned[0] + turned[1] + turned[2]
        return grad + normalise_back(back * slope_all[layer], n_all[layer], scale_all[layer, 0:1, :])

    lax.fori_loop(0, LAYERS, backward, grad)

    for chunk in range(STEP_CHUNKS):
        place_chunk(chunk)


def logderiv_rows(spin, embedding, kernels, readout):
    vmem = pl.BlockSpec(memory_space=pltpu.VMEM)
    hbm = pl.BlockSpec(memory_space=pl.ANY)
    return pl.pallas_call(
        logderiv_kernel,
        out_shape=jax.ShapeDtypeStruct((NS, SEND_SUB, SEND_LANES), jnp.int16),
        in_specs=[vmem, vmem, vmem, hbm],
        out_specs=vmem,
        scratch_shapes=[
            pltpu.VMEM((LAYERS, TAPS * CH, CH), F32),
            pltpu.VMEM((LAYERS, WIDE, SITES), BF16),
            pltpu.VMEM((LAYERS, WIDE, SITES), BF16),
            pltpu.VMEM((LAYERS, CH, SITES), F32),
            pltpu.VMEM((LAYERS, CH, SITES), F32),
            pltpu.VMEM((LAYERS, 8, SITES), F32),
            pltpu.VMEM((LAYERS * LAYER_ROWS + 8, 128), F32),
            pltpu.VMEM((2, CH, 128), F32),
            pltpu.SemaphoreType.DMA((LAYERS,)),
        ],
        compiler_params=pltpu.CompilerParams(vmem_limit_bytes=60 << 20),
        name="logderiv",
    )(spin, embedding, readout, kernels.reshape(LAYERS, TAPS * CH, CH))


def gram_kernel(x_ref, centered_ref, gram_ref, values):
    lower = lax.broadcasted_iota(jnp.int32, (2 * SEND_SUB, 128), 0) < SEND_SUB

    def widen(block, carry):
        for j in range(4):
            first = block * 8 + 2 * j
            both = jnp.concatenate([x_ref[first + i].astype(jnp.int32).astype(F32) for i in range(2)], 0)
            code = both[:, SEND_LANES - 128 :]
            code = jnp.where(lower, code[SEND_SUB - 1 : SEND_SUB], code[2 * SEND_SUB - 1 : 2 * SEND_SUB])
            scale = decode_scale(code) * (1.0 / TOP)
            place = pl.ds(pl.multiple_of(first * SEND_SUB, 8), 2 * SEND_SUB)
            for t in range(SEND_TILES):
                values[t, place, :] = both[:, 128 * t : 128 * t + 128] * scale
        return carry

    lax.fori_loop(0, NS // 8, widen, 0)
    total = jnp.zeros((NS, NS), F32)
    held = None
    for r in range(OWN_ROWS):
        entries = values[r // SEND_SUB, pl.ds(r % SEND_SUB, NS, stride=SEND_SUB), :]
        mean = jnp.sum(entries, axis=0, keepdims=True) * (1.0 / NS)
        centered = ((entries - mean) * (1.0 / math.sqrt(NS))).astype(BF16)
        centered_ref[:, 128 * r : 128 * r + 128] = centered
        if held is None and r + 1 < OWN_ROWS:
            held = centered
        elif held is None:
            total = total + matmul_nt(centered, centered)
        else:
            wide = jnp.concatenate([held, centered], 1)
            total = total + matmul_nt(wide, wide)
            held = None
    gram_ref[:, 0, :] = total


def partial_gram(x):
    vmem = pl.BlockSpec(memory_space=pltpu.VMEM)
    return pl.pallas_call(
        gram_kernel,
        out_shape=(
            jax.ShapeDtypeStruct((NS, OWN_ROWS * 128), BF16),
            jax.ShapeDtypeStruct((NS, 1, NS), F32),
        ),
        in_specs=[vmem],
        out_specs=(vmem, vmem),
        scratch_shapes=[pltpu.VMEM((SEND_TILES, NS * SEND_SUB, 128), F32)],
        compiler_params=pltpu.CompilerParams(vmem_limit_bytes=40 << 20),
        name="partial_gram",
    )(x)


def direction_kernel(table_ref, centered_ref, out_ref, system, r_col, s_col):
    diagonal = lax.broadcasted_iota(jnp.int32, (NS, NS), 0) == lax.broadcasted_iota(
        jnp.int32, (NS, NS), 1
    )

    def total(values):
        return jnp.sum(values, axis=1, keepdims=True)

    def as_column(values):
        return total(jnp.where(diagonal, values, 0.0))

    def as_row(values):
        return jnp.sum(jnp.where(diagonal, values, 0.0), axis=0, keepdims=True)

    gram = table_ref[:, :NS]
    energy = as_row(table_ref[:, NS : NS + 1])
    spread = (energy - total(energy) * (1.0 / NS)) * (1.0 / math.sqrt(NS))
    diag_term = SHIFT_RATIO * (total(as_row(gram)) * (1.0 / NS)) + 1e-06
    system[...] = gram + jnp.where(diagonal, diag_term, 0.0)
    tiny = 1e-37

    def twice(values):
        return jnp.concatenate([values, values], 1)

    def iterate(state):
        count, x, r, p, s, last, alpha, _ = state
        for _ in range(4):
            w_col = total(system[...] * r)
            r_all = r_col[...]
            norm = jnp.sum(r_all * r_all, axis=0, keepdims=True)
            delta = jnp.sum(r_all * w_col, axis=0, keepdims=True)
            beta = norm / jnp.maximum(last, tiny)
            alpha = norm / jnp.maximum(delta - beta * norm / jnp.maximum(alpha, tiny), tiny)
            last = norm
            s_all = w_col + beta * s_col[...]
            s_col[...] = s_all
            r_col[...] = r_all - alpha * s_all
            p = r + twice(beta) * p
            s = as_row(w_col) + twice(beta) * s
            x = x + twice(alpha) * p
            r = r - twice(alpha) * s
        return count + 1, x, r, p, s, last, alpha, norm

    spread_col = jnp.broadcast_to(as_column(spread), (NS, 128))
    r_col[...] = spread_col
    s_col[...] = jnp.zeros((NS, 128), F32)
    start = jnp.sum(spread_col * spread_col, axis=0, keepdims=True)
    goal = start * 1e-13
    zero = jnp.zeros((1, NS), F32)
    _, coeffs, _, _, _, _, _, _ = lax.while_loop(
        lambda state: (state[0] < 512) & ((state[7] - goal)[0, 0] > 0.0),
        iterate,
        (jnp.int32(0), zero, spread, zero, zero, jnp.full((1, 128), 1e30, F32), jnp.ones((1, 128), F32), start),
    )
    square_total = total(coeffs * as_row(total(table_ref[:, :NS] * coeffs)))
    high = coeffs.astype(BF16).astype(F32)
    middle = (coeffs - high).astype(BF16).astype(F32)
    low = coeffs - high - middle
    line = lax.broadcasted_iota(jnp.int32, (16, NS), 0)
    parts = jnp.where(line == 0, high, jnp.where(line == 1, middle, jnp.where(line == 2, low, 0.0)))
    own = jnp.sum(matmul(parts.astype(BF16), centered_ref[...]), axis=0, keepdims=True)
    out_ref[...] = (own * lax.rsqrt(square_total * (1.0 / P_SIZE) + 1e-06))[0]


def direction(table, centered):
    vmem = pl.BlockSpec(memory_space=pltpu.VMEM)
    return pl.pallas_call(
        direction_kernel,
        out_shape=jax.ShapeDtypeStruct((OWN_ROWS * 128,), F32),
        in_specs=[vmem, vmem],
        out_specs=vmem,
        scratch_shapes=[pltpu.VMEM((NS, NS), F32), pltpu.VMEM((NS, 128), F32), pltpu.VMEM((NS, 128), F32)],
        compiler_params=pltpu.CompilerParams(vmem_limit_bytes=40 << 20),
        name="direction",
    )(table, centered)


def exchange(blocks):
    return lax.all_to_all(blocks, "samples", split_axis=0, concat_axis=0, tiled=True)


def per_device(spin_configs, energy, embedding, kernels, readout):
    own = logderiv_rows(spin_configs, embedding, kernels, readout.reshape(1, CH))
    centered, part = partial_gram(exchange(own))
    gram_row = jnp.sum(exchange(part), axis=0)
    line = jnp.concatenate([gram_row, jnp.broadcast_to(energy[:, None], (1, 128))], 1)
    table = exchange(jnp.broadcast_to(line[None], (NS, 1, NS + 128))).reshape(NS, NS + 128)
    return direction(table, centered)


def solution(mesh):
    return jax.shard_map(
        per_device,
        mesh=mesh,
        in_specs=(P("samples", None), P("samples"), P(), P(), P()),
        out_specs=P("samples"),
        check_vma=False,
    )
```

```python
import math

import jax
import jax.numpy as jnp
from jax import lax
from jax.experimental import pallas as pl
from jax.experimental.pallas import tpu as pltpu
from jax.sharding import PartitionSpec as P

SIDE = 16
SITES = 256
HALF = 128
CH = 64
LAYERS = 24
NS = 256
TAPS = 9
STEPS = (1, 0, -1)
WIDE = 192
OWN_ROWS = 27
SEND_SUB = 4
STEP_CHUNKS = 11
SEND_TILES = 7
SEND_LANES = 128 * SEND_TILES
TOP = 32767.0
LAYER_ROWS = 288
P_SIZE = 884736

SHIFT_RATIO = 0.05
GELU_A = math.sqrt(2.0 / math.pi)
GELU_B = 0.044715

F32 = jnp.float32
BF16 = jnp.bfloat16


def split_two(values):
    high = values.astype(BF16)
    low = (values - high.astype(F32)).astype(BF16)
    return high, low


def matmul(a, b):
    return lax.dot_general(a, b, (((1,), (0,)), ((), ())), preferred_element_type=F32)


def matmul_nt(a, b):
    return lax.dot_general(a, b, (((1,), (1,)), ((), ())), preferred_element_type=F32)


def roll_lanes(values, amount):
    return pltpu.roll(values, amount % HALF, 1)


def halves(values):
    return values[:, :HALF], values[:, HALF:]


def join(even, odd):
    return jnp.concatenate([even, odd], 1)


def column_before(odd, place):
    return jnp.where(place == 0, roll_lanes(odd, -7), roll_lanes(odd, 1))


def column_after(even, place):
    return jnp.where(place == 7, roll_lanes(even, 7), roll_lanes(even, -1))


def column_roll(values, step, place):
    even, odd = halves(values)
    if step == 1:
        return join(column_before(odd, place), even)
    if step == -1:
        return join(odd, column_after(even, place))
    return values


def row_roll(values, step):
    if step == 0:
        return values
    even, odd = halves(values)
    return join(roll_lanes(even, 8 * step), roll_lanes(odd, 8 * step))


def normalise(hidden):
    deviation = hidden - jnp.mean(hidden, axis=0, keepdims=True)
    scale = lax.rsqrt(jnp.mean(deviation * deviation, axis=0, keepdims=True) + 1e-05)
    return deviation * scale, scale


def activate(n):
    square = n * n
    t = jnp.tanh(GELU_A * (n + GELU_B * (n * square)))
    half = 0.5 * (1.0 + t)
    slope = half + (0.5 * GELU_A) * n * (1.0 - t * t) * (1.0 + (3.0 * GELU_B) * square)
    return n * half, slope


def normalise_back(grad, n, scale):
    return scale * (
        grad
        - jnp.mean(grad, axis=0, keepdims=True)
        - n * jnp.mean(grad * n, axis=0, keepdims=True)
    )


def encode_scale(largest):
    largest = jnp.maximum(largest, 1e-30)
    exponent = jnp.ceil(jnp.log(largest) * (1.0 / math.log(2.0)) + 0.006)
    mantissa = jnp.ceil(largest * jnp.exp2(-exponent) * 512.0 - 256.0)
    return exponent * 256.0 + jnp.clip(mantissa, 0.0, 255.0)


def decode_scale(code):
    exponent = jnp.floor(code * (1.0 / 256.0))
    return jnp.exp2(exponent) * ((code - 256.0 * exponent + 256.0) * (1.0 / 512.0))


def logderiv_kernel(
    spin_ref, embed_ref, readout_ref, kernels_hbm, out_ref,
    weights, u_hi, u_lo, n_all, slope_all, scale_all, rows, pair, sems,
):
    def fetch(layer):
        return pltpu.make_async_copy(kernels_hbm.at[layer], weights.at[layer], sems.at[layer])

    lax.fori_loop(0, LAYERS, lambda i, c: (fetch(i).start(), c)[1], 0)

    place = lax.broadcasted_iota(jnp.int32, (CH, HALF), 1) & 7
    diagonal = lax.broadcasted_iota(jnp.int32, (CH, CH), 0) == lax.broadcasted_iota(
        jnp.int32, (CH, CH), 1
    )

    def as_column(row):
        return jnp.sum(jnp.where(diagonal, row, 0.0), axis=1, keepdims=True)

    source = lax.broadcasted_iota(jnp.int32, (SITES, SITES), 0)
    target = lax.broadcasted_iota(jnp.int32, (SITES, SITES), 1)
    wanted = ((target & 127) >> 3) * SIDE + 2 * (target & 7) + (target >> 7)
    order = jnp.where(source == wanted, 1.0, 0.0).astype(BF16)
    spin = matmul(jnp.broadcast_to(spin_ref[...].astype(F32), (16, SITES)).astype(BF16), order)[:8]
    hidden = jnp.zeros((CH, SITES), F32)
    for k in range(TAPS):
        copy = row_roll(column_roll(spin, STEPS[k % 3], place[:8]), STEPS[k // 3])
        hidden = hidden + as_column(embed_ref[k : k + 1, :]) * copy[0:1, :]

    def forward(layer, hidden):
        fetch(layer).wait()
        n, scale = normalise(hidden)
        u, slope = activate(n)
        n_all[layer] = n
        slope_all[layer] = slope
        scale_all[layer, 0:1, :] = scale
        for half in range(2):
            pair[half] = u[:, 128 * half : 128 * half + 128]
        mixed = jnp.concatenate(
            [
                jnp.concatenate([pair[half, pl.ds(odd, 32, stride=2), :] for half in range(2)], 1)
                for odd in range(2)
            ],
            0,
        )
        for store, part in zip((u_hi, u_lo), split_two(mixed)):
            for i, step in enumerate(STEPS):
                store[layer, pl.ds(CH * i, CH), :] = row_roll(part, step)
        groups = [
            split_two(
                jnp.concatenate(
                    [
                        weights[layer, pl.ds(CH * (3 * i + j) + odd, 32, stride=2), :]
                        for i in range(3)
                        for odd in range(2)
                    ],
                    0,
                )
            )
            for j in range(3)
        ]
        w_hi, w_lo = [
            jnp.concatenate([group[i].T for group in groups], 0)
            for i in range(2)
        ]
        sums = matmul(w_hi, u_hi[layer]) + (matmul(w_hi, u_lo[layer]) + matmul(w_lo, u_hi[layer]))
        moved = [column_roll(sums[CH * i : CH * i + CH], step, place) for i, step in enumerate(STEPS)]
        return hidden + (moved[0] + moved[1] + moved[2])

    hidden = lax.fori_loop(0, LAYERS, forward, hidden)

    n, scale = normalise(hidden)
    _, slope = activate(n)
    grad = normalise_back((as_column(readout_ref[...]) * (1.0 / SIDE)) * slope, n, scale)
    left = lax.broadcasted_iota(jnp.int32, (32, 128), 1) < CH

    spare = lax.broadcasted_iota(jnp.int32, (SEND_SUB, 128), 0) == SEND_SUB - 1

    def place_chunk(chunk):
        tiles = [rows[pl.ds(chunk * OWN_ROWS + SEND_SUB * t, SEND_SUB), :] for t in range(SEND_TILES)]
        tiles[-1] = jnp.where(spare, 0.0, tiles[-1])
        largest = jnp.abs(tiles[0])
        for tile in tiles[1:]:
            largest = jnp.maximum(largest, jnp.abs(tile))
        code = encode_scale(jnp.max(largest, axis=0, keepdims=True))
        factor = TOP / decode_scale(code)
        coded = [jnp.round(tile * factor) for tile in tiles]
        coded[-1] = jnp.where(spare, code, coded[-1])
        out_ref[chunk] = jnp.concatenate(coded, 1).astype(jnp.int32).astype(jnp.int16)

    def backward(step, grad):
        layer = LAYERS - 1 - step
        first = (LAYER_ROWS * (layer + 1) + OWN_ROWS - 1) // OWN_ROWS
        for j in range(STEP_CHUNKS):
            place_chunk(jnp.minimum(first + j, NS - 1))
        high, low = split_two(grad)
        g_hi, g_lo = [
            jnp.concatenate([column_roll(part, -step, place) for step in STEPS], 0)
            for part in (high, low)
        ]
        w_hi, w_lo = [
            jnp.concatenate(
                [
                    jnp.concatenate([part[CH * (3 * i + j) : CH * (3 * i + j) + CH] for j in range(3)], 1)
                    for i in range(3)
                ],
                0,
            )
            for part in split_two(weights[layer])
        ]
        sums = matmul(w_hi, g_hi) + (matmul(w_hi, g_lo) + matmul(w_lo, g_hi))
        x_hi, x_lo = [jnp.concatenate([part, part[128:]], 0) for part in (g_hi, g_lo)]
        both = matmul_nt(jnp.concatenate([u_hi[layer], u_lo[layer]], 0), x_hi)
        products = both[:WIDE] + (both[WIDE:] + matmul_nt(u_hi[layer], x_lo))
        for i in range(3):
            even, odd = products[CH * i : CH * i + 32], products[CH * i + 32 : CH * i + CH]
            packed = (
                jnp.where(left, even[:, :128], pltpu.roll(odd[:, :128], CH, 1)),
                jnp.where(left, pltpu.roll(even[:, :128], CH, 1), odd[:, :128]),
                jnp.where(left, even[:, 128:], odd[:, 128:]),
            )
            for j in range(3):
                target_rows = pl.multiple_of(layer * LAYER_ROWS + 32 * (3 * i + j), 8)
                rows[pl.ds(target_rows, 32), :] = packed[j]
        turned = [row_roll(sums[CH * i : CH * i + CH], -step) for i, step in enumerate(STEPS)]
        back = turned[0] + turned[1] + turned[2]
        return grad + normalise_back(back * slope_all[layer], n_all[layer], scale_all[layer, 0:1, :])

    lax.fori_loop(0, LAYERS, backward, grad)

    for chunk in range(STEP_CHUNKS):
        place_chunk(chunk)


def logderiv_rows(spin, embedding, kernels, readout):
    vmem = pl.BlockSpec(memory_space=pltpu.VMEM)
    hbm = pl.BlockSpec(memory_space=pl.ANY)
    return pl.pallas_call(
        logderiv_kernel,
        out_shape=jax.ShapeDtypeStruct((NS, SEND_SUB, SEND_LANES), jnp.int16),
        in_specs=[vmem, vmem, vmem, hbm],
        out_specs=vmem,
        scratch_shapes=[
            pltpu.VMEM((LAYERS, TAPS * CH, CH), F32),
            pltpu.VMEM((LAYERS, WIDE, SITES), BF16),
            pltpu.VMEM((LAYERS, WIDE, SITES), BF16),
            pltpu.VMEM((LAYERS, CH, SITES), F32),
            pltpu.VMEM((LAYERS, CH, SITES), F32),
            pltpu.VMEM((LAYERS, 8, SITES), F32),
            pltpu.VMEM((LAYERS * LAYER_ROWS + 8, 128), F32),
            pltpu.VMEM((2, CH, 128), F32),
            pltpu.SemaphoreType.DMA((LAYERS,)),
        ],
        compiler_params=pltpu.CompilerParams(vmem_limit_bytes=60 << 20),
        name="logderiv",
    )(spin, embedding, readout, kernels.reshape(LAYERS, TAPS * CH, CH))


def gram_kernel(x_ref, centered_ref, gram_ref, values):
    lower = lax.broadcasted_iota(jnp.int32, (2 * SEND_SUB, 128), 0) < SEND_SUB

    def widen(block, carry):
        for j in range(4):
            first = block * 8 + 2 * j
            both = jnp.concatenate([x_ref[first + i].astype(jnp.int32).astype(F32) for i in range(2)], 0)
            code = both[:, SEND_LANES - 128 :]
            code = jnp.where(lower, code[SEND_SUB - 1 : SEND_SUB], code[2 * SEND_SUB - 1 : 2 * SEND_SUB])
            scale = decode_scale(code) * (1.0 / TOP)
            place = pl.ds(pl.multiple_of(first * SEND_SUB, 8), 2 * SEND_SUB)
            for t in range(SEND_TILES):
                values[t, place, :] = both[:, 128 * t : 128 * t + 128] * scale
        return carry

    lax.fori_loop(0, NS // 8, widen, 0)
    total = jnp.zeros((NS, NS), F32)
    held = None
    for r in range(OWN_ROWS):
        entries = values[r // SEND_SUB, pl.ds(r % SEND_SUB, NS, stride=SEND_SUB), :]
        mean = jnp.sum(entries, axis=0, keepdims=True) * (1.0 / NS)
        centered = ((entries - mean) * (1.0 / math.sqrt(NS))).astype(BF16)
        centered_ref[:, 128 * r : 128 * r + 128] = centered
        if held is None and r + 1 < OWN_ROWS:
            held = centered
        elif held is None:
            total = total + matmul_nt(centered, centered)
        else:
            wide = jnp.concatenate([held, centered], 1)
            total = total + matmul_nt(wide, wide)
            held = None
    gram_ref[:, 0, :] = total


def partial_gram(x):
    vmem = pl.BlockSpec(memory_space=pltpu.VMEM)
    return pl.pallas_call(
        gram_kernel,
        out_shape=(
            jax.ShapeDtypeStruct((NS, OWN_ROWS * 128), BF16),
            jax.ShapeDtypeStruct((NS, 1, NS), F32),
        ),
        in_specs=[vmem],
        out_specs=(vmem, vmem),
        scratch_shapes=[pltpu.VMEM((SEND_TILES, NS * SEND_SUB, 128), F32)],
        compiler_params=pltpu.CompilerParams(vmem_limit_bytes=40 << 20),
        name="partial_gram",
    )(x)


def spare_column(row):
    return jnp.where(row < NS // 2, row + (NS // 2 - 1), row - NS // 2)


def direction_kernel(table_ref, centered_ref, out_ref, system, gram_full, r_col, s_col):
    diagonal = lax.broadcasted_iota(jnp.int32, (NS, NS), 0) == lax.broadcasted_iota(
        jnp.int32, (NS, NS), 1
    )

    def total(values):
        return jnp.sum(values, axis=1, keepdims=True)

    def as_column(values):
        return total(jnp.where(diagonal, values, 0.0))

    def as_row(values):
        return jnp.sum(jnp.where(diagonal, values, 0.0), axis=0, keepdims=True)

    row = lax.broadcasted_iota(jnp.int32, (NS, NS), 0)
    column = lax.broadcasted_iota(jnp.int32, (NS, NS), 1)
    table = table_ref[...]
    spare = column == spare_column(row)
    energy = as_row(total(jnp.where(spare, table, 0.0)))
    mirrored = jnp.sum(jnp.where(row == spare_column(column), table, 0.0), axis=0, keepdims=True)
    gram = jnp.where(spare, as_column(mirrored), table)
    gram_full[...] = gram
    spread = (energy - total(energy) * (1.0 / NS)) * (1.0 / math.sqrt(NS))
    diag_term = SHIFT_RATIO * (total(as_row(gram)) * (1.0 / NS)) + 1e-06
    system[...] = gram + jnp.where(diagonal, diag_term, 0.0)
    tiny = 1e-37

    def twice(values):
        return jnp.concatenate([values, values], 1)

    def iterate(state):
        count, x, r, p, s, last, alpha, _ = state
        for _ in range(4):
            w_col = total(system[...] * r)
            r_all = r_col[...]
            norm = jnp.sum(r_all * r_all, axis=0, keepdims=True)
            delta = jnp.sum(r_all * w_col, axis=0, keepdims=True)
            beta = norm / jnp.maximum(last, tiny)
            alpha = norm / jnp.maximum(delta - beta * norm / jnp.maximum(alpha, tiny), tiny)
            last = norm
            s_all = w_col + beta * s_col[...]
            s_col[...] = s_all
            r_col[...] = r_all - alpha * s_all
            p = r + twice(beta) * p
            s = as_row(w_col) + twice(beta) * s
            x = x + twice(alpha) * p
            r = r - twice(alpha) * s
        return count + 1, x, r, p, s, last, alpha, norm

    spread_col = jnp.broadcast_to(as_column(spread), (NS, 128))
    r_col[...] = spread_col
    s_col[...] = jnp.zeros((NS, 128), F32)
    start = jnp.sum(spread_col * spread_col, axis=0, keepdims=True)
    goal = start * 1e-13
    zero = jnp.zeros((1, NS), F32)
    _, coeffs, _, _, _, _, _, _ = lax.while_loop(
        lambda state: (state[0] < 512) & ((state[7] - goal)[0, 0] > 0.0),
        iterate,
        (jnp.int32(0), zero, spread, zero, zero, jnp.full((1, 128), 1e30, F32), jnp.ones((1, 128), F32), start),
    )
    square_total = total(coeffs * as_row(total(gram_full[...] * coeffs)))
    high = coeffs.astype(BF16).astype(F32)
    middle = (coeffs - high).astype(BF16).astype(F32)
    low = coeffs - high - middle
    line = lax.broadcasted_iota(jnp.int32, (16, NS), 0)
    parts = jnp.where(line == 0, high, jnp.where(line == 1, middle, jnp.where(line == 2, low, 0.0)))
    own = jnp.sum(matmul(parts.astype(BF16), centered_ref[...]), axis=0, keepdims=True)
    out_ref[...] = (own * lax.rsqrt(square_total * (1.0 / P_SIZE) + 1e-06))[0]


def direction(table, centered):
    vmem = pl.BlockSpec(memory_space=pltpu.VMEM)
    return pl.pallas_call(
        direction_kernel,
        out_shape=jax.ShapeDtypeStruct((OWN_ROWS * 128,), F32),
        in_specs=[vmem, vmem],
        out_specs=vmem,
        scratch_shapes=[pltpu.VMEM((NS, NS), F32), pltpu.VMEM((NS, NS), F32), pltpu.VMEM((NS, 128), F32), pltpu.VMEM((NS, 128), F32)],
        compiler_params=pltpu.CompilerParams(vmem_limit_bytes=40 << 20),
        name="direction",
    )(table, centered)


def exchange(blocks):
    return lax.all_to_all(blocks, "samples", split_axis=0, concat_axis=0, tiled=True)


def per_device(spin_configs, energy, embedding, kernels, readout):
    own = logderiv_rows(spin_configs, embedding, kernels, readout.reshape(1, CH))
    centered, part = partial_gram(exchange(own))
    gram_row = jnp.sum(exchange(part), axis=0)
    at_spare = jnp.arange(NS) == spare_column(lax.axis_index("samples"))
    line = jnp.where(at_spare, energy[0], gram_row)
    table = exchange(jnp.broadcast_to(line[None], (NS, 1, NS))).reshape(NS, NS)
    return direction(table, centered)


def solution(mesh):
    return jax.shard_map(
        per_device,
        mesh=mesh,
        in_specs=(P("samples", None), P("samples"), P(), P(), P()),
        out_specs=P("samples"),
        check_vma=False,
    )
```

```python
import math

import jax
import jax.numpy as jnp
from jax import lax
from jax.experimental import pallas as pl
from jax.experimental.pallas import tpu as pltpu
from jax.sharding import PartitionSpec as P

SIDE = 16
SITES = 256
HALF = 128
CH = 64
LAYERS = 24
NS = 256
TAPS = 9
STEPS = (1, 0, -1)
WIDE = 192
OWN_ROWS = 27
SEND_SUB = 4
STEP_CHUNKS = 11
SEND_TILES = 7
SEND_LANES = 128 * SEND_TILES
TOP = 32767.0
LAYER_ROWS = 288
P_SIZE = 884736

SHIFT_RATIO = 0.05
GELU_A = math.sqrt(2.0 / math.pi)
GELU_B = 0.044715

F32 = jnp.float32
BF16 = jnp.bfloat16


def split_two(values):
    high = values.astype(BF16)
    low = (values - high.astype(F32)).astype(BF16)
    return high, low


def matmul(a, b):
    return lax.dot_general(a, b, (((1,), (0,)), ((), ())), preferred_element_type=F32)


def matmul_nt(a, b):
    return lax.dot_general(a, b, (((1,), (1,)), ((), ())), preferred_element_type=F32)


def roll_lanes(values, amount):
    return pltpu.roll(values, amount % HALF, 1)


def halves(values):
    return values[:, :HALF], values[:, HALF:]


def join(even, odd):
    return jnp.concatenate([even, odd], 1)


def column_before(odd, place):
    return jnp.where(place == 0, roll_lanes(odd, -7), roll_lanes(odd, 1))


def column_after(even, place):
    return jnp.where(place == 7, roll_lanes(even, 7), roll_lanes(even, -1))


def column_roll(values, step, place):
    even, odd = halves(values)
    if step == 1:
        return join(column_before(odd, place), even)
    if step == -1:
        return join(odd, column_after(even, place))
    return values


def row_roll(values, step):
    if step == 0:
        return values
    even, odd = halves(values)
    return join(roll_lanes(even, 8 * step), roll_lanes(odd, 8 * step))


def normalise(hidden):
    deviation = hidden - jnp.mean(hidden, axis=0, keepdims=True)
    scale = lax.rsqrt(jnp.mean(deviation * deviation, axis=0, keepdims=True) + 1e-05)
    return deviation * scale, scale


def activate(n):
    square = n * n
    t = jnp.tanh(GELU_A * (n + GELU_B * (n * square)))
    half = 0.5 * (1.0 + t)
    slope = half + (0.5 * GELU_A) * n * (1.0 - t * t) * (1.0 + (3.0 * GELU_B) * square)
    return n * half, slope


def normalise_back(grad, n, scale):
    return scale * (
        grad
        - jnp.mean(grad, axis=0, keepdims=True)
        - n * jnp.mean(grad * n, axis=0, keepdims=True)
    )


def encode_scale(largest):
    largest = jnp.maximum(largest, 1e-30)
    exponent = jnp.ceil(jnp.log(largest) * (1.0 / math.log(2.0)) + 0.006)
    mantissa = jnp.ceil(largest * jnp.exp2(-exponent) * 512.0 - 256.0)
    return exponent * 256.0 + jnp.clip(mantissa, 0.0, 255.0)


def decode_scale(code):
    exponent = jnp.floor(code * (1.0 / 256.0))
    return jnp.exp2(exponent) * ((code - 256.0 * exponent + 256.0) * (1.0 / 512.0))


def logderiv_kernel(
    spin_ref, embed_ref, readout_ref, kernels_hbm, out_ref,
    weights, u_hi, u_lo, n_all, slope_all, scale_all, rows, pair, sems,
):
    def fetch(layer):
        return pltpu.make_async_copy(kernels_hbm.at[layer], weights.at[layer], sems.at[layer])

    lax.fori_loop(0, LAYERS, lambda i, c: (fetch(i).start(), c)[1], 0)

    place = lax.broadcasted_iota(jnp.int32, (CH, HALF), 1) & 7
    diagonal = lax.broadcasted_iota(jnp.int32, (CH, CH), 0) == lax.broadcasted_iota(
        jnp.int32, (CH, CH), 1
    )

    def as_column(row):
        return jnp.sum(jnp.where(diagonal, row, 0.0), axis=1, keepdims=True)

    source = lax.broadcasted_iota(jnp.int32, (SITES, SITES), 0)
    target = lax.broadcasted_iota(jnp.int32, (SITES, SITES), 1)
    wanted = ((target & 127) >> 3) * SIDE + 2 * (target & 7) + (target >> 7)
    order = jnp.where(source == wanted, 1.0, 0.0).astype(BF16)
    spin = matmul(jnp.broadcast_to(spin_ref[...].astype(F32), (16, SITES)).astype(BF16), order)[:8]
    hidden = jnp.zeros((CH, SITES), F32)
    for k in range(TAPS):
        copy = row_roll(column_roll(spin, STEPS[k % 3], place[:8]), STEPS[k // 3])
        hidden = hidden + as_column(embed_ref[k : k + 1, :]) * copy[0:1, :]

    def forward(layer, hidden):
        fetch(layer).wait()
        n, scale = normalise(hidden)
        u, slope = activate(n)
        n_all[layer] = n
        slope_all[layer] = slope
        scale_all[layer, 0:1, :] = scale
        for half in range(2):
            pair[half] = u[:, 128 * half : 128 * half + 128]
        mixed = jnp.concatenate(
            [
                jnp.concatenate([pair[half, pl.ds(odd, 32, stride=2), :] for half in range(2)], 1)
                for odd in range(2)
            ],
            0,
        )
        for store, part in zip((u_hi, u_lo), split_two(mixed)):
            for i, step in enumerate(STEPS):
                store[layer, pl.ds(CH * i, CH), :] = row_roll(part, step)
        groups = [
            split_two(
                jnp.concatenate(
                    [
                        weights[layer, pl.ds(CH * (3 * i + j) + odd, 32, stride=2), :]
                        for i in range(3)
                        for odd in range(2)
                    ],
                    0,
                )
            )
            for j in range(3)
        ]
        w_hi, w_lo = [
            jnp.concatenate([group[i].T for group in groups], 0)
            for i in range(2)
        ]
        stacked = matmul(jnp.concatenate([w_hi, w_lo], 0), u_hi[layer])
        sums = stacked[:WIDE] + (stacked[WIDE:] + matmul(w_hi, u_lo[layer]))
        moved = [column_roll(sums[CH * i : CH * i + CH], step, place) for i, step in enumerate(STEPS)]
        return hidden + (moved[0] + moved[1] + moved[2])

    hidden = lax.fori_loop(0, LAYERS, forward, hidden)

    n, scale = normalise(hidden)
    _, slope = activate(n)
    grad = normalise_back((as_column(readout_ref[...]) * (1.0 / SIDE)) * slope, n, scale)
    left = lax.broadcasted_iota(jnp.int32, (32, 128), 1) < CH

    spare = lax.broadcasted_iota(jnp.int32, (SEND_SUB, 128), 0) == SEND_SUB - 1

    def place_chunk(chunk):
        tiles = [rows[pl.ds(chunk * OWN_ROWS + SEND_SUB * t, SEND_SUB), :] for t in range(SEND_TILES)]
        tiles[-1] = jnp.where(spare, 0.0, tiles[-1])
        largest = jnp.abs(tiles[0])
        for tile in tiles[1:]:
            largest = jnp.maximum(largest, jnp.abs(tile))
        code = encode_scale(jnp.max(largest, axis=0, keepdims=True))
        factor = TOP / decode_scale(code)
        coded = [jnp.round(tile * factor) for tile in tiles]
        coded[-1] = jnp.where(spare, code, coded[-1])
        out_ref[chunk] = jnp.concatenate(coded, 1).astype(jnp.int32).astype(jnp.int16)

    def backward(step, grad):
        layer = LAYERS - 1 - step
        first = (LAYER_ROWS * (layer + 1) + OWN_ROWS - 1) // OWN_ROWS
        for j in range(STEP_CHUNKS):
            place_chunk(jnp.minimum(first + j, NS - 1))
        high, low = split_two(grad)
        g_hi, g_lo = [
            jnp.concatenate([column_roll(part, -step, place) for step in STEPS], 0)
            for part in (high, low)
        ]
        w_hi, w_lo = [
            jnp.concatenate(
                [
                    jnp.concatenate([part[CH * (3 * i + j) : CH * (3 * i + j) + CH] for j in range(3)], 1)
                    for i in range(3)
                ],
                0,
            )
            for part in split_two(weights[layer])
        ]
        stacked = matmul(jnp.concatenate([w_hi, w_lo], 0), g_hi)
        sums = stacked[:WIDE] + (stacked[WIDE:] + matmul(w_hi, g_lo))
        x_hi, x_lo = [jnp.concatenate([part, part[128:]], 0) for part in (g_hi, g_lo)]
        both = matmul_nt(jnp.concatenate([u_hi[layer], u_lo[layer]], 0), x_hi)
        products = both[:WIDE] + (both[WIDE:] + matmul_nt(u_hi[layer], x_lo))
        for i in range(3):
            even, odd = products[CH * i : CH * i + 32], products[CH * i + 32 : CH * i + CH]
            packed = (
                jnp.where(left, even[:, :128], pltpu.roll(odd[:, :128], CH, 1)),
                jnp.where(left, pltpu.roll(even[:, :128], CH, 1), odd[:, :128]),
                jnp.where(left, even[:, 128:], odd[:, 128:]),
            )
            for j in range(3):
                target_rows = pl.multiple_of(layer * LAYER_ROWS + 32 * (3 * i + j), 8)
                rows[pl.ds(target_rows, 32), :] = packed[j]
        turned = [row_roll(sums[CH * i : CH * i + CH], -step) for i, step in enumerate(STEPS)]
        back = turned[0] + turned[1] + turned[2]
        return grad + normalise_back(back * slope_all[layer], n_all[layer], scale_all[layer, 0:1, :])

    lax.fori_loop(0, LAYERS, backward, grad)

    for chunk in range(STEP_CHUNKS):
        place_chunk(chunk)


def logderiv_rows(spin, embedding, kernels, readout):
    vmem = pl.BlockSpec(memory_space=pltpu.VMEM)
    hbm = pl.BlockSpec(memory_space=pl.ANY)
    return pl.pallas_call(
        logderiv_kernel,
        out_shape=jax.ShapeDtypeStruct((NS, SEND_SUB, SEND_LANES), jnp.int16),
        in_specs=[vmem, vmem, vmem, hbm],
        out_specs=vmem,
        scratch_shapes=[
            pltpu.VMEM((LAYERS, TAPS * CH, CH), F32),
            pltpu.VMEM((LAYERS, WIDE, SITES), BF16),
            pltpu.VMEM((LAYERS, WIDE, SITES), BF16),
            pltpu.VMEM((LAYERS, CH, SITES), F32),
            pltpu.VMEM((LAYERS, CH, SITES), F32),
            pltpu.VMEM((LAYERS, 8, SITES), F32),
            pltpu.VMEM((LAYERS * LAYER_ROWS + 8, 128), F32),
            pltpu.VMEM((2, CH, 128), F32),
            pltpu.SemaphoreType.DMA((LAYERS,)),
        ],
        compiler_params=pltpu.CompilerParams(vmem_limit_bytes=60 << 20),
        name="logderiv",
    )(spin, embedding, readout, kernels.reshape(LAYERS, TAPS * CH, CH))


def gram_kernel(x_ref, centered_ref, gram_ref, values):
    lower = lax.broadcasted_iota(jnp.int32, (2 * SEND_SUB, 128), 0) < SEND_SUB

    def widen(block, carry):
        for j in range(4):
            first = block * 8 + 2 * j
            both = jnp.concatenate([x_ref[first + i].astype(jnp.int32).astype(F32) for i in range(2)], 0)
            code = both[:, SEND_LANES - 128 :]
            code = jnp.where(lower, code[SEND_SUB - 1 : SEND_SUB], code[2 * SEND_SUB - 1 : 2 * SEND_SUB])
            scale = decode_scale(code) * (1.0 / TOP)
            place = pl.ds(pl.multiple_of(first * SEND_SUB, 8), 2 * SEND_SUB)
            for t in range(SEND_TILES):
                values[t, place, :] = both[:, 128 * t : 128 * t + 128] * scale
        return carry

    lax.fori_loop(0, NS // 8, widen, 0)
    total = jnp.zeros((NS, NS), F32)
    held = None
    for r in range(OWN_ROWS):
        entries = values[r // SEND_SUB, pl.ds(r % SEND_SUB, NS, stride=SEND_SUB), :]
        mean = jnp.sum(entries, axis=0, keepdims=True) * (1.0 / NS)
        centered = ((entries - mean) * (1.0 / math.sqrt(NS))).astype(BF16)
        centered_ref[:, 128 * r : 128 * r + 128] = centered
        if held is None and r + 1 < OWN_ROWS:
            held = centered
        elif held is None:
            total = total + matmul_nt(centered, centered)
        else:
            wide = jnp.concatenate([held, centered], 1)
            total = total + matmul_nt(wide, wide)
            held = None
    gram_ref[:, 0, :] = total


def partial_gram(x):
    vmem = pl.BlockSpec(memory_space=pltpu.VMEM)
    return pl.pallas_call(
        gram_kernel,
        out_shape=(
            jax.ShapeDtypeStruct((NS, OWN_ROWS * 128), BF16),
            jax.ShapeDtypeStruct((NS, 1, NS), F32),
        ),
        in_specs=[vmem],
        out_specs=(vmem, vmem),
        scratch_shapes=[pltpu.VMEM((SEND_TILES, NS * SEND_SUB, 128), F32)],
        compiler_params=pltpu.CompilerParams(vmem_limit_bytes=40 << 20),
        name="partial_gram",
    )(x)


def spare_column(row):
    return jnp.where(row < NS // 2, row + (NS // 2 - 1), row - NS // 2)


def direction_kernel(table_ref, centered_ref, out_ref, system, gram_full, r_col, s_col):
    diagonal = lax.broadcasted_iota(jnp.int32, (NS, NS), 0) == lax.broadcasted_iota(
        jnp.int32, (NS, NS), 1
    )

    def total(values):
        return jnp.sum(values, axis=1, keepdims=True)

    def as_column(values):
        return total(jnp.where(diagonal, values, 0.0))

    def as_row(values):
        return jnp.sum(jnp.where(diagonal, values, 0.0), axis=0, keepdims=True)

    row = lax.broadcasted_iota(jnp.int32, (NS, NS), 0)
    column = lax.broadcasted_iota(jnp.int32, (NS, NS), 1)
    table = table_ref[...]
    spare = column == spare_column(row)
    energy = as_row(total(jnp.where(spare, table, 0.0)))
    mirrored = jnp.sum(jnp.where(row == spare_column(column), table, 0.0), axis=0, keepdims=True)
    gram = jnp.where(spare, as_column(mirrored), table)
    gram_full[...] = gram
    spread = (energy - total(energy) * (1.0 / NS)) * (1.0 / math.sqrt(NS))
    diag_term = SHIFT_RATIO * (total(as_row(gram)) * (1.0 / NS)) + 1e-06
    system[...] = gram + jnp.where(diagonal, diag_term, 0.0)
    tiny = 1e-37

    def twice(values):
        return jnp.concatenate([values, values], 1)

    def iterate(state):
        count, x, r, p, s, last, alpha, _ = state
        for _ in range(6):
            w_col = total(system[...] * r)
            r_all = r_col[...]
            norm = jnp.sum(r_all * r_all, axis=0, keepdims=True)
            delta = jnp.sum(r_all * w_col, axis=0, keepdims=True)
            beta = norm / jnp.maximum(last, tiny)
            alpha = norm / jnp.maximum(delta - beta * norm / jnp.maximum(alpha, tiny), tiny)
            last = norm
            s_all = w_col + beta * s_col[...]
            s_col[...] = s_all
            r_col[...] = r_all - alpha * s_all
            p = r + twice(beta) * p
            s = as_row(w_col) + twice(beta) * s
            x = x + twice(alpha) * p
            r = r - twice(alpha) * s
        return count + 1, x, r, p, s, last, alpha, norm

    spread_col = jnp.broadcast_to(as_column(spread), (NS, 128))
    r_col[...] = spread_col
    s_col[...] = jnp.zeros((NS, 128), F32)
    start = jnp.sum(spread_col * spread_col, axis=0, keepdims=True)
    goal = start * 1e-13
    zero = jnp.zeros((1, NS), F32)
    _, coeffs, _, _, _, _, _, _ = lax.while_loop(
        lambda state: (state[0] < 512) & ((state[7] - goal)[0, 0] > 0.0),
        iterate,
        (jnp.int32(0), zero, spread, zero, zero, jnp.full((1, 128), 1e30, F32), jnp.ones((1, 128), F32), start),
    )
    square_total = total(coeffs * as_row(total(gram_full[...] * coeffs)))
    high = coeffs.astype(BF16).astype(F32)
    middle = (coeffs - high).astype(BF16).astype(F32)
    low = coeffs - high - middle
    line = lax.broadcasted_iota(jnp.int32, (16, NS), 0)
    parts = jnp.where(line == 0, high, jnp.where(line == 1, middle, jnp.where(line == 2, low, 0.0)))
    own = jnp.sum(matmul(parts.astype(BF16), centered_ref[...]), axis=0, keepdims=True)
    out_ref[...] = (own * lax.rsqrt(square_total * (1.0 / P_SIZE) + 1e-06))[0]


def direction(table, centered):
    vmem = pl.BlockSpec(memory_space=pltpu.VMEM)
    return pl.pallas_call(
        direction_kernel,
        out_shape=jax.ShapeDtypeStruct((OWN_ROWS * 128,), F32),
        in_specs=[vmem, vmem],
        out_specs=vmem,
        scratch_shapes=[pltpu.VMEM((NS, NS), F32), pltpu.VMEM((NS, NS), F32), pltpu.VMEM((NS, 128), F32), pltpu.VMEM((NS, 128), F32)],
        compiler_params=pltpu.CompilerParams(vmem_limit_bytes=40 << 20),
        name="direction",
    )(table, centered)


def exchange(blocks):
    return lax.all_to_all(blocks, "samples", split_axis=0, concat_axis=0, tiled=True)


def per_device(spin_configs, energy, embedding, kernels, readout):
    own = logderiv_rows(spin_configs, embedding, kernels, readout.reshape(1, CH))
    centered, part = partial_gram(exchange(own))
    gram_row = jnp.sum(exchange(part), axis=0)
    at_spare = jnp.arange(NS) == spare_column(lax.axis_index("samples"))
    line = jnp.where(at_spare, energy[0], gram_row)
    table = exchange(jnp.broadcast_to(line[None], (NS, 1, NS))).reshape(NS, NS)
    return direction(table, centered)


def solution(mesh):
    return jax.shard_map(
        per_device,
        mesh=mesh,
        in_specs=(P("samples", None), P("samples"), P(), P(), P()),
        out_specs=P("samples"),
        check_vma=False,
    )
```
